32 devices in a mesh: row: 4 (over z), col: 8 (over y, x, core).
Axes of the slice: x: 2, y: 2, z: 4, core: 2. Of those that a mesh axis runs over, the one named last changes fastest.
Arguments:
- a_vals: bfloat16 [4, 8, 4, 8, 128, 128], P('row', 'col'), may hold values from -0.5 to 0.5
- a_rows: int32 [4, 8, 4, 8], P('row', 'col'), may hold values from 0 to 15
- a_cols: int32 [4, 8, 4, 8], P('row', 'col'), may hold values from 0 to 1
- a_live: int32 [4, 8, 4], P('row', 'col'), may hold values from 1 to 8, as said below
- p_vals: bfloat16 [64, 3, 128, 128], P(('row', 'col')), may hold values from -1 to 1
- p_cols: int32 [64, 3], replicated, may hold values from 0 to 15, as said below
Outputs:
- coarse_op: float32 [16, 16, 128, 128], P('col', 'row')
The draws below stay inside these ranges and needn't reach their ends.
Inputs may be any that keep to these rules, and one draw needn't show every extreme that they name: Only slots t < a_live[r, c, s] carry blocks of A; the values in the other slots are not part of A. In every draw some grid position has all its sections full. `p_cols`: the 3 coarse block columns of a fine block row i are distinct and lie in the 4 coarse blocks from (i // 16) * 4 on.
All inputs are finite; a program needn't handle non-finite values.
Results may differ from the reference program's by a relative error of at most 0.0029.
Values may be sent and summed in bfloat16 or wider, within the bound.
No kernel may reach another device: no remote copies, remote signals or barrier semaphores. Data moves between devices by JAX's collectives and lax.ppermute only.
A program may use at most 128 MiB of HBM per device.

```python
import jax
import jax.numpy as jnp
from jax import lax

BS = 128
KP = 3
CROW = 4
SEG = 2
SLOTS = 8
SECTIONS = 4
GRID_COLS = 8
FROWS = 16
NF = 64
NC = 16


def draw_a_live(key, part):
    heavy_key = jax.random.fold_in(key, 11)
    pick_key = jax.random.fold_in(key, 12)
    count_key = jax.random.fold_in(key, 13)
    chosen = jax.random.randint(pick_key, (), 0, SECTIONS * GRID_COLS)
    device = jnp.arange(SECTIONS)[:, None] * GRID_COLS + jnp.arange(GRID_COLS)[None, :]
    heavy = (jax.random.randint(heavy_key, (SECTIONS, GRID_COLS), 0, 8) == 0) | (device == chosen)
    light_counts = 1 + jax.random.randint(count_key, (SECTIONS, GRID_COLS, SECTIONS), 0, max(SLOTS // 3, 1))
    return jnp.where(heavy[:, :, None], SLOTS, light_counts).astype(jnp.int32)


def draw_p_cols(key, part):
    scores = jax.random.randint(jax.random.fold_in(key, 21), (NF, CROW), 0, 1 << 20) * CROW + jnp.arange(CROW)[None, :]
    chosen = jnp.argsort(scores, axis=1)[:, :KP]
    offsets = jnp.arange(NF) // FROWS * CROW
    return (chosen + offsets[:, None]).astype(jnp.int32)


def with_ends(values, stream_key, low, largest):
    dims = values.shape
    place = [jax.random.randint(jax.random.fold_in(stream_key, axis), (), 0, dims[axis]) for axis in range(len(dims))]
    values = values.at[tuple(place)].set(low)
    longest = dims.index(max(dims))
    place[longest] = (place[longest] + 1) % dims[longest]
    return values.at[tuple(place)].set(largest)


def levels(stream_key, shape, shards, least, high):
    gain = 1.0
    for axis_at, blocks in shards:
        steps = jax.random.uniform(jax.random.fold_in(jax.random.fold_in(stream_key, 6), axis_at), (blocks,), jnp.float32, least / len(shards), high / len(shards))
        gain = gain * jnp.repeat(jnp.exp(steps), shape[axis_at] // blocks).reshape((-1,) + (1,) * (len(shape) - 1 - axis_at))
    return gain


def bell_draw(stream_key, shape, width, most, split=(), kind=jnp.bfloat16):
    loudness = levels(stream_key, shape, split, -0.22, 0.18) if split else 1.0
    drawn = jax.random.normal(stream_key, shape, jnp.float32) * width * loudness
    return jnp.minimum(jnp.maximum(drawn, -most), most).astype(kind)


def setup_inputs(seed: int = 0) -> dict:
    key_list = jax.random.split(jax.random.key(seed), 7)
    return {
        "a_vals": bell_draw(key_list[0], (SECTIONS, GRID_COLS, SECTIONS, SLOTS, BS, BS), BS ** -0.5, 0.5, ((0, 4), (1, 8))),
        "a_rows": with_ends(jax.random.randint(key_list[1], (SECTIONS, GRID_COLS, SECTIONS, SLOTS), 0, FROWS), jax.random.fold_in(key_list[1], 1), 0, FROWS - 1).astype(jnp.int32),
        "a_cols": with_ends(jax.random.randint(key_list[2], (SECTIONS, GRID_COLS, SECTIONS, SLOTS), 0, SEG), jax.random.fold_in(key_list[2], 1), 0, SEG - 1).astype(jnp.int32),
        "a_live": draw_a_live(jax.random.fold_in(key_list[6], 71), 0),
        "p_vals": bell_draw(key_list[4], (NF, KP, BS, BS), 0.16, 1.0, ((0, 32),)),
        "p_cols": draw_p_cols(jax.random.fold_in(key_list[6], 71), 0),
    }


def reference(a_vals, a_rows, a_cols, a_live, p_vals, p_cols):
    global_tables = (p_vals, p_cols)
    return assemble(a_vals, a_rows, a_cols, a_live, global_tables)


def assemble(a_vals, a_rows, a_cols, a_live, global_tables):
    p_vals, p_cols = global_tables

    def per_row(inputs):
        values, fine_rows, fine_cols, live_count, row_index = inputs
        section_ids = jnp.arange(SECTIONS, dtype=jnp.int32)[None, :, None]
        column_ids = jnp.arange(GRID_COLS, dtype=jnp.int32)[:, None, None]
        position = jnp.arange(SLOTS, dtype=jnp.int32)[None, None, :]
        target = ((section_ids * GRID_COLS + column_ids) * SEG + fine_cols).astype(jnp.int32)
        usable = position < live_count[:, :, None]
        right_blocks = p_vals[target]
        products = jnp.einsum("crsij,crspjk->crspik", values.astype(jnp.float32), right_blocks.astype(jnp.float32), precision=lax.Precision.HIGHEST)
        products = jnp.where(usable[..., None, None, None], products, 0.0).astype(jnp.bfloat16)
        coarse_col = p_cols[target]
        row_spread = jnp.broadcast_to(fine_rows[..., None], coarse_col.shape)
        gathered = jnp.zeros((FROWS, NC, BS, BS), jnp.float32).at[row_spread, coarse_col].add(products.astype(jnp.float32))
        first_row = (row_index * FROWS).astype(jnp.int32)
        left_blocks = lax.dynamic_slice_in_dim(p_vals, first_row, FROWS, 0).astype(jnp.float32)
        coarse_row = lax.dynamic_slice_in_dim(p_cols, first_row, FROWS, 0) - row_index * CROW
        selector = (coarse_row[:, :, None] == jnp.arange(CROW, dtype=jnp.int32)[None, None, :]).astype(jnp.float32)
        mixed = jnp.einsum("iaq,iamn->qimn", selector, left_blocks, precision=lax.Precision.HIGHEST)
        return jnp.einsum("qimn,ijmk->jqnk", mixed, gathered, precision=lax.Precision.HIGHEST)

    row_numbers = jnp.arange(SECTIONS, dtype=jnp.int32)
    blocks = lax.map(per_row, (a_vals, a_rows, a_cols, a_live, row_numbers))
    return jnp.transpose(blocks, (1, 0, 2, 3, 4)).reshape(NC, NC, BS, BS)
```

```python
import functools

import jax
import jax.numpy as jnp
from jax import lax
from jax.experimental import pallas as pl
from jax.experimental.pallas import tpu as pltpu
from jax.sharding import PartitionSpec as P

CROW = 4
HALF = 2


def fold_left(sizes, info, pcols, *refs):
    pieces, out = refs[:-1], refs[-1]
    _, segment, per_row, block = sizes
    grid_row, grid_col = info[0], info[1]
    fine_span = segment * len(pieces)
    for b, piece in enumerate(pieces):
        for seg in range(segment):
            i = lax.bitwise_xor(grid_col, b) * segment + seg
            base = (grid_row * fine_span + i) * per_row
            used = 0
            for q in range(per_row):
                coarse = pcols[base + q] - grid_row * CROW
                used = used + coarse
                out[i, coarse] = jnp.transpose(piece[seg, q])
            out[i, CROW * (CROW - 1) // 2 - used] = jnp.zeros((block, block), out.dtype)


def section(sizes, hop, info, pcols, own_a, other_a, left, *refs):
    slots, segment, per_row, block = sizes
    pieces, (out, a_buf, r_buf, folded, lhs, rhs, sems) = refs[:-7], refs[-7:]
    row_count = len(pieces) // 2
    grid_row, grid_col = info[0], info[1]
    chip, core = grid_col // 2, grid_col % 2
    sec = lax.bitwise_xor(chip, hop)
    dist = lax.bitwise_xor(sec, grid_row)
    copies = [
        pltpu.make_async_copy(own_a.at[sec], a_buf.at[0], sems.at[0]),
        pltpu.make_async_copy(other_a.at[sec], a_buf.at[1], sems.at[1]),
    ]
    for copy in copies:
        copy.start()
    for d in range(row_count):

        @pl.when(dist == d)
        def _():
            two = [
                pltpu.make_async_copy(pieces[2 * d + u], r_buf.at[u], sems.at[2 + u])
                for u in range(2)
            ]
            for copy in two:
                copy.start()
            for copy in two:
                copy.wait()

    for u in range(2):
        col = lax.bitwise_xor(grid_col, u)
        for seg in range(segment):
            k = (sec * 2 * row_count + col) * segment + seg
            cols = [pcols[k * per_row + p] for p in range(per_row)]
            for jj in range(HALF):
                want = sec * CROW + core * HALF + jj
                at = jnp.int32(0)
                found = cols[0] == want
                for p in range(1, per_row):
                    at = jnp.where(cols[p] == want, p, at)
                    found = found | (cols[p] == want)
                blk = r_buf[u, seg, at]
                folded[u * segment + seg, :, jj * block : (jj + 1) * block] = jnp.where(
                    found, blk, jnp.zeros_like(blk)
                )
    for copy in copies:
        copy.wait()
    for u in range(2):
        for t in range(slots):
            code = info[2 + (u * row_count + sec) * slots + t]
            live = code >= 0
            code = jnp.maximum(code, 0)
            n = u * slots + t
            product = jnp.dot(
                a_buf[u, t],
                folded[u * segment + code % segment],
                preferred_element_type=jnp.float32,
            )
            rhs[n * block : (n + 1) * block, :] = jnp.where(live, product, 0.0).astype(rhs.dtype)
            lhs[:, n * block : (n + 1) * block] = left[code // segment].reshape(CROW * block, block)
    acc = jnp.dot(lhs[...], rhs[...], preferred_element_type=jnp.float32)
    for jj in range(HALF):
        for i in range(CROW):
            out[jj, i] = acc[
                i * block : (i + 1) * block, jj * block : (jj + 1) * block
            ].astype(out.dtype)


def local(a_vals, a_rows, a_cols, a_live, p_vals, p_cols):
    row_count = lax.axis_size("row")
    col_count = lax.axis_size("col")
    assert col_count == 2 * row_count
    grid_row = lax.axis_index("row")
    grid_col = lax.axis_index("col")
    segment, per_row, block = p_vals.shape[0], p_vals.shape[1], p_vals.shape[2]
    slots = a_vals.shape[3]
    sizes = (slots, segment, per_row, block)

    def col_xor(x, b):
        return lax.ppermute(x, "col", [(c, c ^ b) for c in range(col_count)])

    def row_xor(x, b):
        return lax.ppermute(x, "row", [(r, r ^ b) for r in range(row_count)])

    own_a = a_vals.reshape(row_count, slots, block, block)
    position = lax.iota(jnp.int32, slots)[None, :]
    codes = jnp.where(
        position < a_live.reshape(row_count, 1),
        a_rows.reshape(row_count, slots) * segment + a_cols.reshape(row_count, slots),
        -1,
    )
    right_far = [row_xor(p_vals, d) for d in range(1, row_count)]
    left_far = [col_xor(p_vals, 2 * e) for e in range(1, row_count)]
    other_p = col_xor(p_vals, 1)
    other_a = col_xor(own_a, 1)
    other_codes = col_xor(codes, 1)
    left = [p_vals, other_p]
    for piece in left_far:
        left += [piece, col_xor(piece, 1)]
    right = [p_vals, other_p]
    for piece in right_far:
        right += [piece, col_xor(piece, 1)]
    info = jnp.concatenate(
        [jnp.stack([grid_row, grid_col]), codes.reshape(-1), other_codes.reshape(-1)]
    )
    pcols = p_cols.reshape(-1)
    smem = pl.BlockSpec(memory_space=pltpu.SMEM)
    vmem = pl.BlockSpec(memory_space=pltpu.VMEM)
    hbm = pl.BlockSpec(memory_space=pl.ANY)
    fine = segment * col_count
    folded_left = pl.pallas_call(
        functools.partial(fold_left, sizes),
        out_shape=jax.ShapeDtypeStruct((fine, CROW, block, block), jnp.bfloat16),
        in_specs=[smem, smem] + [vmem] * col_count,
        out_specs=vmem,
        compiler_params=pltpu.CompilerParams(vmem_limit_bytes=16 << 20),
        cost_estimate=pl.CostEstimate(flops=0, bytes_accessed=4 << 20, transcendentals=0),
        name="fold_left",
    )(info, pcols, *left)
    depth = 2 * slots * block

    def partial_of(hop, dtype):
        return pl.pallas_call(
            functools.partial(section, sizes, hop),
            out_shape=jax.ShapeDtypeStruct((HALF, CROW, block, block), dtype),
            in_specs=[smem, smem, hbm, hbm, vmem] + [hbm] * len(right),
            out_specs=vmem,
            scratch_shapes=[
                pltpu.VMEM((2, slots, block, block), jnp.bfloat16),
                pltpu.VMEM((2, segment, per_row, block, block), jnp.bfloat16),
                pltpu.VMEM((2 * segment, block, HALF * block), jnp.bfloat16),
                pltpu.VMEM((CROW * block, depth), jnp.bfloat16),
                pltpu.VMEM((depth, HALF * block), jnp.bfloat16),
                pltpu.SemaphoreType.DMA((4,)),
            ],
            compiler_params=pltpu.CompilerParams(vmem_limit_bytes=24 << 20),
            cost_estimate=pl.CostEstimate(
                flops=2 * CROW * block * depth * HALF * block,
                bytes_accessed=4 << 20,
                transcendentals=0,
            ),
            name="section",
        )(info, pcols, own_a, other_a, folded_left, *right)

    arrived = []
    for hop in range(row_count - 1, 0, -1):
        arrived.append(col_xor(partial_of(hop, jnp.bfloat16), 2 * hop))
    total = partial_of(0, jnp.float32)
    for piece in arrived:
        total = total + piece.astype(jnp.float32)
    return total


def solution(mesh):
    return jax.shard_map(
        local,
        mesh=mesh,
        in_specs=(
            P("row", "col", None, None, None, None),
            P("row", "col", None, None),
            P("row", "col", None, None),
            P("row", "col", None),
            P(("row", "col"), None, None, None),
            P(),
        ),
        out_specs=P("col", "row", None, None),
        check_vma=False,
    )
```

```python
import functools

import jax
import jax.numpy as jnp
from jax import lax
from jax.experimental import pallas as pl
from jax.experimental.pallas import tpu as pltpu
from jax.sharding import PartitionSpec as P

CROW = 4
HALF = 2


def fold_left(sizes, hop, info, *refs):
    pieces, out = refs[:2], refs[-1]
    slots, segment, per_row, block = sizes
    table = 2 + slots * out.shape[0] // segment
    grid_row, grid_col = info[0], info[1]
    for u, piece in enumerate(pieces):
        for seg in range(segment):
            i = lax.bitwise_xor(grid_col, 2 * hop + u) * segment + seg
            base = table + (grid_row * out.shape[0] + i) * per_row
            used = 0
            for q in range(per_row):
                coarse = info[base + q] - grid_row * CROW
                used = used + coarse
                out[i, coarse] = jnp.transpose(piece[seg, q])
            out[i, CROW * (CROW - 1) // 2 - used] = jnp.zeros((block, block), out.dtype)


def section(sizes, hop, info, own_a, other_a, left, *refs):
    slots, segment, per_row, block = sizes
    pieces, (out, folded, lhs, rhs) = refs[:-4], refs[-4:]
    row_count = len(pieces) // 2
    table = 2 + slots * len(pieces)
    grid_row, grid_col = info[0], info[1]
    chip, core = grid_col // 2, grid_col % 2
    sec = lax.bitwise_xor(chip, hop)
    dist = lax.bitwise_xor(sec, grid_row)
    for d in range(row_count):

        @pl.when(dist == d)
        def _():
            for u in range(2):
                col = lax.bitwise_xor(grid_col, u)
                for seg in range(segment):
                    k = (sec * 2 * row_count + col) * segment + seg
                    cols = [info[table + k * per_row + p] for p in range(per_row)]
                    for jj in range(HALF):
                        want = sec * CROW + core * HALF + jj
                        at = jnp.int32(0)
                        found = cols[0] == want
                        for p in range(1, per_row):
                            at = jnp.where(cols[p] == want, p, at)
                            found = found | (cols[p] == want)
                        blk = pieces[2 * d + u][seg, at]
                        folded[u * segment + seg, :, jj * block : (jj + 1) * block] = jnp.where(
                            found, blk, jnp.zeros_like(blk)
                        )

    for u in range(2):
        for t in range(slots):
            code = info[2 + (u * row_count + sec) * slots + t]
            live = code >= 0
            code = jnp.maximum(code, 0)
            n = u * slots + t
            product = jnp.dot(
                (own_a, other_a)[u][sec, t],
                folded[u * segment + code % segment],
                preferred_element_type=jnp.float32,
            )
            rhs[n * block : (n + 1) * block, :] = jnp.where(live, product, 0.0).astype(rhs.dtype)
            lhs[:, n * block : (n + 1) * block] = left[code // segment].reshape(CROW * block, block)
    acc = jnp.dot(lhs[...], rhs[...], preferred_element_type=jnp.float32)
    for jj in range(HALF):
        for i in range(CROW):
            out[jj, i] = acc[
                i * block : (i + 1) * block, jj * block : (jj + 1) * block
            ].astype(out.dtype)


def local(a_vals, a_rows, a_cols, a_live, p_vals, p_cols):
    row_count = lax.axis_size("row")
    col_count = lax.axis_size("col")
    assert col_count == 2 * row_count
    grid_row = lax.axis_index("row")
    grid_col = lax.axis_index("col")
    segment, per_row, block = p_vals.shape[0], p_vals.shape[1], p_vals.shape[2]
    slots = a_vals.shape[3]
    sizes = (slots, segment, per_row, block)

    def col_xor(x, b):
        return lax.ppermute(x, "col", [(c, c ^ b) for c in range(col_count)])

    def row_xor(x, b):
        return lax.ppermute(x, "row", [(r, r ^ b) for r in range(row_count)])

    own_a = a_vals.reshape(row_count, slots, block, block)
    position = lax.iota(jnp.int32, slots)[None, :]
    codes = jnp.where(
        position < a_live.reshape(row_count, 1),
        a_rows.reshape(row_count, slots) * segment + a_cols.reshape(row_count, slots),
        -1,
    )
    right = [p_vals] + [None] * (row_count - 1)
    for d in sorted(range(1, row_count), key=lambda d: (d.bit_count(), -d)):
        right[d] = row_xor(right[d & (d - 1)], d & -d)
    other_codes = col_xor(codes, 1)
    info = jnp.concatenate(
        [
            jnp.stack([grid_row, grid_col]),
            codes.reshape(-1),
            other_codes.reshape(-1),
            p_cols.reshape(-1),
        ]
    )
    near_p, info, other_p, other_a = lax.optimization_barrier(
        (p_vals, info, col_xor(p_vals, 1), col_xor(own_a, 1))
    )
    left = [p_vals] + [col_xor(near_p, 2 * e) for e in range(1, row_count)]
    right = [half for piece in right[1:] for half in (piece, col_xor(piece, 1))]
    right = [p_vals, other_p] + right
    smem = pl.BlockSpec(memory_space=pltpu.SMEM)
    vmem = pl.BlockSpec(memory_space=pltpu.VMEM)
    hbm = pl.BlockSpec(memory_space=pl.ANY)
    folded_left = ()
    for hop in [*range(1, row_count), 0]:
        pair = (left[hop], col_xor(left[hop], 1) if hop else other_p)
        folded_left = (
            pl.pallas_call(
                functools.partial(fold_left, sizes, hop),
                out_shape=jax.ShapeDtypeStruct(
                    (segment * col_count, CROW, block, block), jnp.bfloat16
                ),
                in_specs=[smem, vmem, vmem] + [hbm] * len(folded_left),
                out_specs=vmem,
                input_output_aliases={3: 0} if folded_left else {},
                compiler_params=pltpu.CompilerParams(vmem_limit_bytes=8 << 20),
                cost_estimate=pl.CostEstimate(
                    flops=0, bytes_accessed=1 << 20, transcendentals=0
                ),
                name="fold_left",
            )(info, *pair, *folded_left),
        )
    (folded_left,) = folded_left
    depth = 2 * slots * block

    def partial_of(hop, dtype):
        return pl.pallas_call(
            functools.partial(section, sizes, hop),
            out_shape=jax.ShapeDtypeStruct((HALF, CROW, block, block), dtype),
            in_specs=[smem] + [vmem] * (3 + len(right)),
            out_specs=vmem,
            scratch_shapes=[
                pltpu.VMEM((2 * segment, block, HALF * block), jnp.bfloat16),
                pltpu.VMEM((CROW * block, depth), jnp.bfloat16),
                pltpu.VMEM((depth, HALF * block), jnp.bfloat16),
            ],
            compiler_params=pltpu.CompilerParams(vmem_limit_bytes=16 << 20),
            cost_estimate=pl.CostEstimate(
                flops=2 * CROW * block * depth * HALF * block,
                bytes_accessed=4 << 20,
                transcendentals=0,
            ),
            name="section",
        )(info, own_a, other_a, folded_left, *right)

    arrived = []
    for hop in range(row_count - 1, 0, -1):
        arrived.append(col_xor(partial_of(hop, jnp.bfloat16), 2 * hop))
    total = partial_of(0, jnp.float32)
    for piece in arrived:
        total = total + piece.astype(jnp.float32)
    return total


def solution(mesh):
    return jax.shard_map(
        local,
        mesh=mesh,
        in_specs=(
            P("row", "col", None, None, None, None),
            P("row", "col", None, None),
            P("row", "col", None, None),
            P("row", "col", None),
            P(("row", "col"), None, None, None),
            P(),
        ),
        out_specs=P("col", "row", None, None),
        check_vma=False,
    )
```

```python
import functools

import jax
import jax.numpy as jnp
from jax import lax
from jax.experimental import pallas as pl
from jax.experimental.pallas import tpu as pltpu
from jax.sharding import PartitionSpec as P

CROW = 4
HALF = 2


def fold_left(sizes, hop, info, *refs):
    pieces, out = refs[:2], refs[-1]
    slots, segment, per_row, block = sizes
    table = 2 + slots * out.shape[0] // segment
    grid_row, grid_col = info[0], info[1]
    for u, piece in enumerate(pieces):
        for seg in range(segment):
            i = lax.bitwise_xor(grid_col, 2 * hop + u) * segment + seg
            base = table + (grid_row * out.shape[0] + i) * per_row
            used = 0
            for q in range(per_row):
                coarse = info[base + q] - grid_row * CROW
                used = used + coarse
                out[i, coarse] = jnp.transpose(piece[seg, q])
            out[i, CROW * (CROW - 1) // 2 - used] = jnp.zeros((block, block), out.dtype)


def section(sizes, hop, info, own_a, other_a, left, *refs):
    slots, segment, per_row, block = sizes
    pieces, (out, folded, lhs, rhs) = refs[:-4], refs[-4:]
    row_count = len(pieces) // 2
    table = 2 + slots * len(pieces)
    grid_row, grid_col = info[0], info[1]
    chip, core = grid_col // 2, grid_col % 2
    sec = lax.bitwise_xor(chip, hop)
    dist = lax.bitwise_xor(sec, grid_row)
    for d in range(row_count):

        @pl.when(dist == d)
        def _():
            for u in range(2):
                col = lax.bitwise_xor(grid_col, u)
                for seg in range(segment):
                    k = (sec * 2 * row_count + col) * segment + seg
                    cols = [info[table + k * per_row + p] for p in range(per_row)]
                    for jj in range(HALF):
                        want = sec * CROW + core * HALF + jj
                        at = jnp.int32(0)
                        found = cols[0] == want
                        for p in range(1, per_row):
                            at = jnp.where(cols[p] == want, p, at)
                            found = found | (cols[p] == want)
                        blk = pieces[2 * d + u][seg, at]
                        folded[u * segment + seg, :, jj * block : (jj + 1) * block] = jnp.where(
                            found, blk, jnp.zeros_like(blk)
                        )

    for u in range(2):
        for t in range(slots):
            code = info[2 + (u * row_count + sec) * slots + t]
            live = code >= 0
            code = jnp.maximum(code, 0)
            n = u * slots + t
            product = jnp.dot(
                (own_a, other_a)[u][sec, t],
                folded[u * segment + code % segment],
                preferred_element_type=jnp.float32,
            )
            rhs[n * block : (n + 1) * block, :] = jnp.where(live, product, 0.0).astype(rhs.dtype)
            lhs[:, n * block : (n + 1) * block] = left[code // segment].reshape(CROW * block, block)
    acc = jnp.dot(lhs[...], rhs[...], preferred_element_type=jnp.float32)
    for jj in range(HALF):
        for i in range(CROW):
            out[jj, i] = acc[
                i * block : (i + 1) * block, jj * block : (jj + 1) * block
            ].astype(out.dtype)


def local(a_vals, a_rows, a_cols, a_live, p_vals, p_cols):
    row_count = lax.axis_size("row")
    col_count = lax.axis_size("col")
    assert col_count == 2 * row_count
    grid_row = lax.axis_index("row")
    grid_col = lax.axis_index("col")
    segment, per_row, block = p_vals.shape[0], p_vals.shape[1], p_vals.shape[2]
    slots = a_vals.shape[3]
    sizes = (slots, segment, per_row, block)

    def col_xor(x, b):
        return lax.ppermute(x, "col", [(c, c ^ b) for c in range(col_count)])

    def row_xor(x, b):
        return lax.ppermute(x, "row", [(r, r ^ b) for r in range(row_count)])

    own_a = a_vals.reshape(row_count, slots, block, block)
    position = lax.iota(jnp.int32, slots)[None, :]
    codes = jnp.where(
        position < a_live.reshape(row_count, 1),
        a_rows.reshape(row_count, slots) * segment + a_cols.reshape(row_count, slots),
        -1,
    )
    other_codes = col_xor(codes, 1)
    info = jnp.concatenate(
        [
            jnp.stack([grid_row, grid_col]),
            codes.reshape(-1),
            other_codes.reshape(-1),
            p_cols.reshape(-1),
        ]
    )
    near_p, other_a = lax.optimization_barrier((p_vals, col_xor(own_a, 1)))
    left = [p_vals] + [col_xor(near_p, 2 * e) for e in range(1, row_count)]
    right = [p_vals] + [None] * (row_count - 1)
    for d in sorted(range(1, row_count), key=lambda d: (d.bit_count(), -d)):
        piece = right[d & (d - 1)]
        if d & (d - 1):
            piece, info = lax.optimization_barrier((piece, info))
        right[d] = row_xor(piece, d & -d)
    late_p, *_ = lax.optimization_barrier((p_vals, *left[1:], right[1]))
    other_p = col_xor(late_p, 1)
    right = [half for piece in right[1:] for half in (piece, col_xor(piece, 1))]
    right = [p_vals, other_p] + right
    smem = pl.BlockSpec(memory_space=pltpu.SMEM)
    vmem = pl.BlockSpec(memory_space=pltpu.VMEM)
    hbm = pl.BlockSpec(memory_space=pl.ANY)
    folded_left = ()
    for hop in [*range(1, row_count), 0]:
        pair = (left[hop], col_xor(left[hop], 1) if hop else other_p)
        folded_left = (
            pl.pallas_call(
                functools.partial(fold_left, sizes, hop),
                out_shape=jax.ShapeDtypeStruct(
                    (segment * col_count, CROW, block, block), jnp.bfloat16
                ),
                in_specs=[smem, vmem, vmem] + [hbm] * len(folded_left),
                out_specs=vmem,
                input_output_aliases={3: 0} if folded_left else {},
                compiler_params=pltpu.CompilerParams(vmem_limit_bytes=8 << 20),
                cost_estimate=pl.CostEstimate(
                    flops=0, bytes_accessed=1 << 20, transcendentals=0
                ),
                name="fold_left",
            )(info, *pair, *folded_left),
        )
    (folded_left,) = folded_left
    depth = 2 * slots * block

    def partial_of(hop, dtype):
        return pl.pallas_call(
            functools.partial(section, sizes, hop),
            out_shape=jax.ShapeDtypeStruct((HALF, CROW, block, block), dtype),
            in_specs=[smem] + [vmem] * (3 + len(right)),
            out_specs=vmem,
            scratch_shapes=[
                pltpu.VMEM((2 * segment, block, HALF * block), jnp.bfloat16),
                pltpu.VMEM((CROW * block, depth), jnp.bfloat16),
                pltpu.VMEM((depth, HALF * block), jnp.bfloat16),
            ],
            compiler_params=pltpu.CompilerParams(vmem_limit_bytes=16 << 20),
            cost_estimate=pl.CostEstimate(
                flops=2 * CROW * block * depth * HALF * block,
                bytes_accessed=4 << 20,
                transcendentals=0,
            ),
            name="section",
        )(info, own_a, other_a, folded_left, *right)

    arrived = []
    for hop in range(row_count - 1, 0, -1):
        arrived.append(col_xor(partial_of(hop, jnp.bfloat16), 2 * hop))
    total = partial_of(0, jnp.float32)
    for piece in arrived:
        total = total + piece.astype(jnp.float32)
    return total


def solution(mesh):
    return jax.shard_map(
        local,
        mesh=mesh,
        in_specs=(
            P("row", "col", None, None, None, None),
            P("row", "col", None, None),
            P("row", "col", None, None),
            P("row", "col", None),
            P(("row", "col"), None, None, None),
            P(),
        ),
        out_specs=P("col", "row", None, None),
        check_vma=False,
    )
```

```python
import functools

import jax
import jax.numpy as jnp
from jax import lax
from jax.experimental import pallas as pl
from jax.experimental.pallas import tpu as pltpu
from jax.sharding import PartitionSpec as P

CROW = 4
HALF = 2


def fold_left(sizes, hops, info, *refs):
    pieces, out = refs[: 2 * len(hops)], refs[-1]
    slots, segment, per_row, block = sizes
    table = 2 + slots * out.shape[0] // segment
    grid_row, grid_col = info[0], info[1]
    for b, piece in enumerate(pieces):
        for seg in range(segment):
            i = lax.bitwise_xor(grid_col, 2 * hops[b // 2] + b % 2) * segment + seg
            base = table + (grid_row * out.shape[0] + i) * per_row
            used = 0
            for q in range(per_row):
                coarse = info[base + q] - grid_row * CROW
                used = used + coarse
                out[i, coarse] = jnp.transpose(piece[seg, q])
            out[i, CROW * (CROW - 1) // 2 - used] = jnp.zeros((block, block), out.dtype)


def section(sizes, hop, info, own_a, other_a, left, *refs):
    slots, segment, per_row, block = sizes
    pieces, (out, folded, lhs, rhs) = refs[:-4], refs[-4:]
    row_count = len(pieces) // 2
    table = 2 + slots * len(pieces)
    grid_row, grid_col = info[0], info[1]
    chip, core = grid_col // 2, grid_col % 2
    sec = lax.bitwise_xor(chip, hop)
    dist = lax.bitwise_xor(sec, grid_row)
    for d in range(row_count):

        @pl.when(dist == d)
        def _():
            for u in range(2):
                col = lax.bitwise_xor(grid_col, u)
                for seg in range(segment):
                    k = (sec * 2 * row_count + col) * segment + seg
                    cols = [info[table + k * per_row + p] for p in range(per_row)]
                    for jj in range(HALF):
                        want = sec * CROW + core * HALF + jj
                        at = jnp.int32(0)
                        found = cols[0] == want
                        for p in range(1, per_row):
                            at = jnp.where(cols[p] == want, p, at)
                            found = found | (cols[p] == want)
                        blk = pieces[2 * d + u][seg, at]
                        folded[u * segment + seg, :, jj * block : (jj + 1) * block] = jnp.where(
                            found, blk, jnp.zeros_like(blk)
                        )

    for u in range(2):
        for t in range(slots):
            code = info[2 + (u * row_count + sec) * slots + t]
            live = code >= 0
            code = jnp.maximum(code, 0)
            n = u * slots + t
            product = jnp.dot(
                (own_a, other_a)[u][sec, t],
                folded[u * segment + code % segment],
                preferred_element_type=jnp.float32,
            )
            rhs[n * block : (n + 1) * block, :] = jnp.where(live, product, 0.0).astype(rhs.dtype)
            lhs[:, n * block : (n + 1) * block] = left[code // segment].reshape(CROW * block, block)
    acc = jnp.dot(lhs[...], rhs[...], preferred_element_type=jnp.float32)
    for jj in range(HALF):
        for i in range(CROW):
            out[jj, i] = acc[
                i * block : (i + 1) * block, jj * block : (jj + 1) * block
            ].astype(out.dtype)


def local(a_vals, a_rows, a_cols, a_live, p_vals, p_cols):
    row_count = lax.axis_size("row")
    col_count = lax.axis_size("col")
    assert col_count == 2 * row_count
    grid_row = lax.axis_index("row")
    grid_col = lax.axis_index("col")
    segment, per_row, block = p_vals.shape[0], p_vals.shape[1], p_vals.shape[2]
    slots = a_vals.shape[3]
    sizes = (slots, segment, per_row, block)

    def col_xor(x, b):
        return lax.ppermute(x, "col", [(c, c ^ b) for c in range(col_count)])

    def row_xor(x, b):
        return lax.ppermute(x, "row", [(r, r ^ b) for r in range(row_count)])

    own_a = a_vals.reshape(row_count, slots, block, block)
    position = lax.iota(jnp.int32, slots)[None, :]
    codes = lax.optimization_barrier(
        jnp.where(
            position < a_live.reshape(row_count, 1),
            a_rows.reshape(row_count, slots) * segment + a_cols.reshape(row_count, slots),
            -1,
        )
    )
    other_codes = col_xor(codes, 1)
    info = jnp.concatenate(
        [
            jnp.stack([grid_row, grid_col]),
            codes.reshape(-1),
            other_codes.reshape(-1),
            p_cols.reshape(-1),
        ]
    )
    near_p, other_a = lax.optimization_barrier((p_vals, col_xor(own_a, 1)))
    left = [p_vals] + [col_xor(near_p, 2 * e) for e in range(1, row_count)]
    right = [p_vals] + [None] * (row_count - 1)
    for d in sorted(range(1, row_count), key=lambda d: (d.bit_count(), -d)):
        piece = right[d & (d - 1)]
        if d & (d - 1):
            piece, info = lax.optimization_barrier((piece, info))
        right[d] = row_xor(piece, d & -d)
    late_p, *_ = lax.optimization_barrier((p_vals, *left[1:], right[1]))
    other_p = col_xor(late_p, 1)
    right = [half for piece in right[1:] for half in (piece, col_xor(piece, 1))]
    right = [p_vals, other_p] + right
    smem = pl.BlockSpec(memory_space=pltpu.SMEM)
    vmem = pl.BlockSpec(memory_space=pltpu.VMEM)
    hbm = pl.BlockSpec(memory_space=pl.ANY)
    folded_left = ()
    for hops in (range(1, row_count), range(1)):
        halves = [
            half
            for hop in hops
            for half in (left[hop], col_xor(left[hop], 1) if hop else other_p)
        ]
        folded_left = (
            pl.pallas_call(
                functools.partial(fold_left, sizes, hops),
                out_shape=jax.ShapeDtypeStruct(
                    (segment * col_count, CROW, block, block), jnp.bfloat16
                ),
                in_specs=[smem] + [vmem] * len(halves) + [hbm] * len(folded_left),
                out_specs=vmem,
                input_output_aliases={1 + len(halves): 0} if folded_left else {},
                compiler_params=pltpu.CompilerParams(vmem_limit_bytes=16 << 20),
                cost_estimate=pl.CostEstimate(
                    flops=0, bytes_accessed=1 << 20, transcendentals=0
                ),
                name="fold_left",
            )(info, *halves, *folded_left),
        )
    (folded_left,) = folded_left
    depth = 2 * slots * block

    def partial_of(hop, dtype):
        return pl.pallas_call(
            functools.partial(section, sizes, hop),
            out_shape=jax.ShapeDtypeStruct((HALF, CROW, block, block), dtype),
            in_specs=[smem] + [vmem] * (3 + len(right)),
            out_specs=vmem,
            scratch_shapes=[
                pltpu.VMEM((2 * segment, block, HALF * block), jnp.bfloat16),
                pltpu.VMEM((CROW * block, depth), jnp.bfloat16),
                pltpu.VMEM((depth, HALF * block), jnp.bfloat16),
            ],
            compiler_params=pltpu.CompilerParams(vmem_limit_bytes=16 << 20),
            cost_estimate=pl.CostEstimate(
                flops=2 * CROW * block * depth * HALF * block,
                bytes_accessed=4 << 20,
                transcendentals=0,
            ),
            name="section",
        )(info, own_a, other_a, folded_left, *right)

    arrived = []
    for hop in range(1, row_count):
        arrived.append(col_xor(partial_of(hop, jnp.bfloat16), 2 * hop))
    total = partial_of(0, jnp.float32)
    for piece in arrived:
        total = total + piece.astype(jnp.float32)
    return total


def solution(mesh):
    return jax.shard_map(
        local,
        mesh=mesh,
        in_specs=(
            P("row", "col", None, None, None, None),
            P("row", "col", None, None),
            P("row", "col", None, None),
            P("row", "col", None),
            P(("row", "col"), None, None, None),
            P(),
        ),
        out_specs=P("col", "row", None, None),
        check_vma=False,
    )
```

```python
import functools

import jax
import jax.numpy as jnp
from jax import lax
from jax.experimental import pallas as pl
from jax.experimental.pallas import tpu as pltpu
from jax.sharding import PartitionSpec as P

CROW = 4
HALF = 2


def fold_left(sizes, hops, info, *refs):
    pieces, out = refs[: 2 * len(hops)], refs[-1]
    slots, segment, per_row, block = sizes
    table = 2 + slots * out.shape[0] // segment
    grid_row, grid_col = info[0], info[1]
    for b, piece in enumerate(pieces):
        for seg in range(segment):
            i = lax.bitwise_xor(grid_col, 2 * hops[b // 2] + b % 2) * segment + seg
            base = table + (grid_row * out.shape[0] + i) * per_row
            used = 0
            for q in range(per_row):
                coarse = info[base + q] - grid_row * CROW
                used = used + coarse
                out[i, coarse] = jnp.transpose(piece[seg, q])
            out[i, CROW * (CROW - 1) // 2 - used] = jnp.zeros((block, block), out.dtype)


def section(sizes, hop, info, own_a, other_a, left, *refs):
    slots, segment, per_row, block = sizes
    pieces, (out, folded, lhs, rhs) = refs[:-4], refs[-4:]
    row_count = len(pieces) // 2
    table = 2 + slots * len(pieces)
    grid_row, grid_col = info[0], info[1]
    chip, core = grid_col // 2, grid_col % 2
    sec = lax.bitwise_xor(chip, hop)
    dist = lax.bitwise_xor(sec, grid_row)
    for d in range(row_count):

        @pl.when(dist == d)
        def _():
            for u in range(2):
                col = lax.bitwise_xor(grid_col, u)
                for seg in range(segment):
                    k = (sec * 2 * row_count + col) * segment + seg
                    cols = [info[table + k * per_row + p] for p in range(per_row)]
                    for jj in range(HALF):
                        want = sec * CROW + core * HALF + jj
                        at = jnp.int32(0)
                        found = cols[0] == want
                        for p in range(1, per_row):
                            at = jnp.where(cols[p] == want, p, at)
                            found = found | (cols[p] == want)
                        blk = pieces[2 * d + u][seg, at]
                        folded[u * segment + seg, :, jj * block : (jj + 1) * block] = jnp.where(
                            found, blk, jnp.zeros_like(blk)
                        )

    for u in range(2):
        for t in range(slots):
            code = info[2 + (u * row_count + sec) * slots + t]
            live = code >= 0
            code = jnp.maximum(code, 0)
            n = u * slots + t
            product = jnp.dot(
                (own_a, other_a)[u][sec, t],
                folded[u * segment + code % segment],
                preferred_element_type=jnp.float32,
            )
            rhs[n * block : (n + 1) * block, :] = jnp.where(live, product, 0.0).astype(rhs.dtype)
            lhs[:, n * block : (n + 1) * block] = left[code // segment].reshape(CROW * block, block)
    acc = jnp.dot(lhs[...], rhs[...], preferred_element_type=jnp.float32)
    for jj in range(HALF):
        for i in range(CROW):
            out[jj, i] = acc[
                i * block : (i + 1) * block, jj * block : (jj + 1) * block
            ].astype(out.dtype)


def local(a_vals, a_rows, a_cols, a_live, p_vals, p_cols):
    row_count = lax.axis_size("row")
    col_count = lax.axis_size("col")
    assert col_count == 2 * row_count
    grid_row = lax.axis_index("row")
    grid_col = lax.axis_index("col")
    segment, per_row, block = p_vals.shape[0], p_vals.shape[1], p_vals.shape[2]
    slots = a_vals.shape[3]
    sizes = (slots, segment, per_row, block)

    def col_xor(x, b):
        return lax.ppermute(x, "col", [(c, c ^ b) for c in range(col_count)])

    def row_xor(x, b):
        return lax.ppermute(x, "row", [(r, r ^ b) for r in range(row_count)])

    own_a = a_vals.reshape(row_count, slots, block, block)
    position = lax.iota(jnp.int32, slots)[None, :]
    codes = lax.optimization_barrier(
        jnp.where(
            position < a_live.reshape(row_count, 1),
            a_rows.reshape(row_count, slots) * segment + a_cols.reshape(row_count, slots),
            -1,
        )
    )
    other_codes = col_xor(codes, 1)
    info = jnp.concatenate(
        [
            jnp.stack([grid_row, grid_col]),
            codes.reshape(-1),
            other_codes.reshape(-1),
            p_cols.reshape(-1),
        ]
    )
    near_p, other_a = lax.optimization_barrier((p_vals, col_xor(own_a, 1)))
    left = [p_vals] + [col_xor(near_p if e > 1 else p_vals, 2 * e) for e in range(1, row_count)]
    right = [p_vals] + [None] * (row_count - 1)
    for d in sorted(range(1, row_count), key=lambda d: (d.bit_count(), -d)):
        piece = right[d & (d - 1)]
        if d & (d - 1):
            piece, info = lax.optimization_barrier((piece, info))
        right[d] = row_xor(piece, d & -d)
    late_p, *_ = lax.optimization_barrier((p_vals, *left[1:], right[1]))
    other_p = col_xor(late_p, 1)
    right = [half for piece in right[1:] for half in (piece, col_xor(piece, 1))]
    right = [p_vals, other_p] + right
    smem = pl.BlockSpec(memory_space=pltpu.SMEM)
    vmem = pl.BlockSpec(memory_space=pltpu.VMEM)
    hbm = pl.BlockSpec(memory_space=pl.ANY)
    folded_left = ()
    for hops in (range(1, row_count), range(1)):
        halves = [
            half
            for hop in hops
            for half in (left[hop], col_xor(left[hop], 1) if hop else other_p)
        ]
        folded_left = (
            pl.pallas_call(
                functools.partial(fold_left, sizes, hops),
                out_shape=jax.ShapeDtypeStruct(
                    (segment * col_count, CROW, block, block), jnp.bfloat16
                ),
                in_specs=[smem] + [vmem] * len(halves) + [hbm] * len(folded_left),
                out_specs=vmem,
                input_output_aliases={1 + len(halves): 0} if folded_left else {},
                compiler_params=pltpu.CompilerParams(vmem_limit_bytes=16 << 20),
                cost_estimate=pl.CostEstimate(
                    flops=0, bytes_accessed=1 << 20, transcendentals=0
                ),
                name="fold_left",
            )(info, *halves, *folded_left),
        )
    (folded_left,) = folded_left
    depth = 2 * slots * block

    def partial_of(hop, dtype):
        return pl.pallas_call(
            functools.partial(section, sizes, hop),
            out_shape=jax.ShapeDtypeStruct((HALF, CROW, block, block), dtype),
            in_specs=[smem] + [vmem] * (3 + len(right)),
            out_specs=vmem,
            scratch_shapes=[
                pltpu.VMEM((2 * segment, block, HALF * block), jnp.bfloat16),
                pltpu.VMEM((CROW * block, depth), jnp.bfloat16),
                pltpu.VMEM((depth, HALF * block), jnp.bfloat16),
            ],
            compiler_params=pltpu.CompilerParams(vmem_limit_bytes=16 << 20),
            cost_estimate=pl.CostEstimate(
                flops=2 * CROW * block * depth * HALF * block,
                bytes_accessed=4 << 20,
                transcendentals=0,
            ),
            name="section",
        )(info, own_a, other_a, folded_left, *right)

    arrived = []
    for hop in range(1, row_count):
        arrived.append(col_xor(partial_of(hop, jnp.bfloat16), 2 * hop))
    total = partial_of(0, jnp.float32)
    for piece in arrived:
        total = total + piece.astype(jnp.float32)
    return total


def solution(mesh):
    return jax.shard_map(
        local,
        mesh=mesh,
        in_specs=(
            P("row", "col", None, None, None, None),
            P("row", "col", None, None),
            P("row", "col", None, None),
            P("row", "col", None),
            P(("row", "col"), None, None, None),
            P(),
        ),
        out_specs=P("col", "row", None, None),
        check_vma=False,
    )
```

```python
import functools

import jax
import jax.numpy as jnp
from jax import lax
from jax.experimental import pallas as pl
from jax.experimental.pallas import tpu as pltpu
from jax.sharding import PartitionSpec as P

CROW = 4
HALF = 2


def fold_left(sizes, hops, info, *refs):
    pieces, out = refs[: 2 * len(hops)], refs[-1]
    slots, segment, per_row, block = sizes
    table = 2 + slots * out.shape[0] // segment
    grid_row, grid_col = info[0], info[1]
    for b, piece in enumerate(pieces):
        for seg in range(segment):
            i = lax.bitwise_xor(grid_col, 2 * hops[b // 2] + b % 2) * segment + seg
            base = table + (grid_row * out.shape[0] + i) * per_row
            used = 0
            for q in range(per_row):
                coarse = info[base + q] - grid_row * CROW
                used = used + coarse
                out[i, coarse] = jnp.transpose(piece[seg, q])
            out[i, CROW * (CROW - 1) // 2 - used] = jnp.zeros((block, block), out.dtype)


def section(sizes, hop, info, own_a, other_a, left, *refs):
    slots, segment, per_row, block = sizes
    pieces, (out, folded, lhs, rhs) = refs[:-4], refs[-4:]
    row_count = len(pieces) // 2
    table = 2 + slots * len(pieces)
    grid_row, grid_col = info[0], info[1]
    chip, core = grid_col // 2, grid_col % 2
    sec = lax.bitwise_xor(chip, hop)
    dist = lax.bitwise_xor(sec, grid_row)
    for d in range(row_count):

        @pl.when(dist == d)
        def _():
            for u in range(2):
                col = lax.bitwise_xor(grid_col, u)
                for seg in range(segment):
                    k = (sec * 2 * row_count + col) * segment + seg
                    cols = [info[table + k * per_row + p] for p in range(per_row)]
                    for jj in range(HALF):
                        want = sec * CROW + core * HALF + jj
                        at = jnp.int32(0)
                        found = cols[0] == want
                        for p in range(1, per_row):
                            at = jnp.where(cols[p] == want, p, at)
                            found = found | (cols[p] == want)
                        blk = pieces[2 * d + u][seg, at]
                        folded[u * segment + seg, :, jj * block : (jj + 1) * block] = jnp.where(
                            found, blk, jnp.zeros_like(blk)
                        )

    for u in range(2):
        for t in range(slots):
            code = info[2 + (u * row_count + sec) * slots + t]
            live = code >= 0
            code = jnp.maximum(code, 0)
            n = u * slots + t
            product = jnp.dot(
                (own_a, other_a)[u][sec, t],
                folded[u * segment + code % segment],
                preferred_element_type=jnp.float32,
            )
            rhs[n * block : (n + 1) * block, :] = jnp.where(live, product, 0.0).astype(rhs.dtype)
            lhs[:, n * block : (n + 1) * block] = left[code // segment].reshape(CROW * block, block)
    acc = jnp.dot(lhs[...], rhs[...], preferred_element_type=jnp.float32)
    for jj in range(HALF):
        for i in range(CROW):
            out[jj, i] = acc[
                i * block : (i + 1) * block, jj * block : (jj + 1) * block
            ].astype(out.dtype)


def local(a_vals, a_rows, a_cols, a_live, p_vals, p_cols):
    row_count = lax.axis_size("row")
    col_count = lax.axis_size("col")
    assert col_count == 2 * row_count
    grid_row = lax.axis_index("row")
    grid_col = lax.axis_index("col")
    segment, per_row, block = p_vals.shape[0], p_vals.shape[1], p_vals.shape[2]
    slots = a_vals.shape[3]
    sizes = (slots, segment, per_row, block)

    def col_xor(x, b):
        return lax.ppermute(x, "col", [(c, c ^ b) for c in range(col_count)])

    def row_xor(x, b):
        return lax.ppermute(x, "row", [(r, r ^ b) for r in range(row_count)])

    own_a = a_vals.reshape(row_count, slots, block, block)
    position = lax.iota(jnp.int32, slots)[None, :]
    codes = lax.optimization_barrier(
        jnp.where(
            position < a_live.reshape(row_count, 1),
            a_rows.reshape(row_count, slots) * segment + a_cols.reshape(row_count, slots),
            -1,
        )
    )
    other_codes = col_xor(codes, 1)
    info = jnp.concatenate(
        [
            jnp.stack([grid_row, grid_col]),
            codes.reshape(-1),
            other_codes.reshape(-1),
            p_cols.reshape(-1),
        ]
    )
    near_p, other_a = lax.optimization_barrier((p_vals, col_xor(own_a, 1)))
    left = [p_vals] + [col_xor(near_p if e < row_count - 1 else p_vals, 2 * e) for e in range(1, row_count)]
    right = [p_vals] + [None] * (row_count - 1)
    for d in sorted(range(1, row_count), key=lambda d: (d.bit_count(), -d)):
        piece = right[d & (d - 1)]
        if d & (d - 1):
            piece, info = lax.optimization_barrier((piece, info))
        right[d] = row_xor(piece, d & -d)
    late_p, *_ = lax.optimization_barrier((p_vals, *left[1:], right[1]))
    other_p = col_xor(late_p, 1)
    right = [half for piece in right[1:] for half in (piece, col_xor(piece, 1))]
    right = [p_vals, other_p] + right
    smem = pl.BlockSpec(memory_space=pltpu.SMEM)
    vmem = pl.BlockSpec(memory_space=pltpu.VMEM)
    hbm = pl.BlockSpec(memory_space=pl.ANY)
    folded_left = ()
    for hops in (range(1, row_count), range(1)):
        halves = [
            half
            for hop in hops
            for half in (left[hop], col_xor(left[hop], 1) if hop else other_p)
        ]
        folded_left = (
            pl.pallas_call(
                functools.partial(fold_left, sizes, hops),
                out_shape=jax.ShapeDtypeStruct(
                    (segment * col_count, CROW, block, block), jnp.bfloat16
                ),
                in_specs=[smem] + [vmem] * len(halves) + [hbm] * len(folded_left),
                out_specs=vmem,
                input_output_aliases={1 + len(halves): 0} if folded_left else {},
                compiler_params=pltpu.CompilerParams(vmem_limit_bytes=16 << 20),
                cost_estimate=pl.CostEstimate(
                    flops=0, bytes_accessed=1 << 20, transcendentals=0
                ),
                name="fold_left",
            )(info, *halves, *folded_left),
        )
    (folded_left,) = folded_left
    depth = 2 * slots * block

    def partial_of(hop, dtype):
        return pl.pallas_call(
            functools.partial(section, sizes, hop),
            out_shape=jax.ShapeDtypeStruct((HALF, CROW, block, block), dtype),
            in_specs=[smem] + [vmem] * (3 + len(right)),
            out_specs=vmem,
            scratch_shapes=[
                pltpu.VMEM((2 * segment, block, HALF * block), jnp.bfloat16),
                pltpu.VMEM((CROW * block, depth), jnp.bfloat16),
                pltpu.VMEM((depth, HALF * block), jnp.bfloat16),
            ],
            compiler_params=pltpu.CompilerParams(vmem_limit_bytes=16 << 20),
            cost_estimate=pl.CostEstimate(
                flops=2 * CROW * block * depth * HALF * block,
                bytes_accessed=4 << 20,
                transcendentals=0,
            ),
            name="section",
        )(info, own_a, other_a, folded_left, *right)

    arrived = []
    for hop in range(1, row_count):
        arrived.append(col_xor(partial_of(hop, jnp.bfloat16), 2 * hop))
    total = partial_of(0, jnp.float32)
    for piece in arrived:
        total = total + piece.astype(jnp.float32)
    return total


def solution(mesh):
    return jax.shard_map(
        local,
        mesh=mesh,
        in_specs=(
            P("row", "col", None, None, None, None),
            P("row", "col", None, None),
            P("row", "col", None, None),
            P("row", "col", None),
            P(("row", "col"), None, None, None),
            P(),
        ),
        out_specs=P("col", "row", None, None),
        check_vma=False,
    )
```
